128 devices in a mesh: space: 8 (over z, x_hi), chaos: 16 (over y, x_lo, core).
Axes of the slice: x: 4 (x_hi: 2, x_lo: 2; x = x_hi * 2 + x_lo), y: 4, z: 4, core: 2. Of those that a mesh axis runs over, the one named last changes fastest.
Arguments:
- velocity: float32 [48, 3, 8, 64, 128], P('chaos', None, 'space')
- base_velocity: float32 [48, 3, 8, 64, 128], P('chaos', None, 'space')
- mode_slot: int32 [35], replicated, may hold values from 0 to 47, as said below
- triples: int32 [4096, 3], replicated, may hold values from 0 to 34, as said below
- triple_coef: bfloat16 [4096], replicated, may hold values from -0.29882812 to 0.29882812
Outputs:
- convection: float32 [48, 3, 8, 64, 128], P('chaos', None, 'space')
- next_velocity: float32 [48, 3, 8, 64, 128], P('chaos', None, 'space')
The draws below stay inside these ranges and needn't reach their ends.
Inputs may be any that keep to these rules, and one draw needn't show every extreme that they name: `mode_slot`: the modes take distinct slots; slots that hold no mode are zero in velocity and base_velocity. `triples`: each triple (i, j, k) of modes is listed at most once.
All inputs are finite; a program needn't handle non-finite values.
Results may differ from the reference program's by a relative error of at most 0.0052.
Values may be sent and summed in bfloat16 or wider, within the bound.
A program may use at most 192 MiB of HBM per device.

```python
import jax
import jax.numpy as jnp
from jax import lax

MODES = 35
SLOTS = 48
NY = 64
NZ = 128
NNZ = 4096
NX = 8


def slot_table(key):
    base_key = jax.random.fold_in(key, 101)
    scores = jax.random.permutation(jax.random.fold_in(base_key, 1), SLOTS).astype(jnp.int32)
    scores = scores.at[0].set(-2).at[SLOTS - 1].set(-1)
    chosen = jnp.argsort(scores, stable=True)[:MODES]
    order = jax.random.permutation(jax.random.fold_in(base_key, 2), MODES)
    return chosen[order].astype(jnp.int32)


def live_field(key, salt):
    slots = slot_table(key)
    live = jnp.zeros((SLOTS,), jnp.float32).at[slots].set(1.0)
    noise_key = jax.random.fold_in(key, salt)
    shape = (SLOTS, 3, NX, NY, NZ)
    values = jax.random.normal(noise_key, shape, jnp.float32)
    scales = jnp.exp(jax.random.uniform(jax.random.fold_in(noise_key, 3), (SLOTS, 3, 1, 1, 1), jnp.float32, -1.0, 0.5))
    return values * scales * live[:, None, None, None, None]


def draw_velocity(key, part):
    return live_field(key, 201)


def draw_base_velocity(key, part):
    return live_field(key, 202)


def draw_mode_slot(key, part):
    return slot_table(key)


def draw_triples(key, part):
    flat_index = jax.random.permutation(jax.random.fold_in(key, 301), MODES * MODES * MODES)[:NNZ]
    return jnp.stack([flat_index // (MODES * MODES), flat_index // MODES % MODES, flat_index % MODES], axis=1).astype(jnp.int32)


def gaussian(own_key, extent, width, most, kind=jnp.bfloat16):
    return jnp.clip(width * jax.random.normal(own_key, extent, jnp.float32), -most, most).astype(kind)


def setup_inputs(seed: int = 0) -> dict:
    splits = jax.random.split(jax.random.key(seed), 6)
    return {
        "velocity": draw_velocity(jax.random.fold_in(splits[5], 71), 0),
        "base_velocity": draw_base_velocity(jax.random.fold_in(splits[5], 71), 0),
        "mode_slot": draw_mode_slot(jax.random.fold_in(splits[5], 71), 0),
        "triples": draw_triples(jax.random.fold_in(splits[5], 71), 0),
        "triple_coef": gaussian(splits[4], (NNZ,), 0.05, 0.29882812),
    }


SECTION_STEP = 0.5


def slopes(padded):
    interior = padded[:, :, 1:-1]
    along_x = 0.5 * (padded[:, :, 2:] - padded[:, :, :-2])
    along_y = 0.5 * (jnp.roll(interior, -1, 3) - jnp.roll(interior, 1, 3))
    along_z = 0.5 * (jnp.roll(interior, -1, 4) - jnp.roll(interior, 1, 4))
    return jnp.stack([along_x, along_y, along_z], axis=2)


def reference(velocity, base_velocity, mode_slot, triples, triple_coef):
    rounded = velocity.astype(jnp.bfloat16)
    moving = rounded.astype(jnp.float32)
    padded = jnp.concatenate([moving[:, :, -1:], moving, moving[:, :, :1]], axis=2)
    gradients = slopes(padded).astype(jnp.bfloat16)
    slot_i = mode_slot[triples[:, 0]].astype(jnp.int32)
    slot_j = mode_slot[triples[:, 1]].astype(jnp.int32)
    slot_k = mode_slot[triples[:, 2]].astype(jnp.int32)
    coef_values = triple_coef.astype(jnp.float32)

    def add_triple(running, entry):
        out_slot, left_slot, right_slot, weight = entry
        term = jnp.sum(moving[left_slot][None] * gradients[right_slot].astype(jnp.float32), axis=1)
        return running.at[out_slot].add(weight * term), None

    start_sum = jnp.zeros(moving.shape, jnp.float32)
    convection, _ = lax.scan(add_triple, start_sum, (slot_k, slot_i, slot_j, coef_values))
    next_velocity = base_velocity - SECTION_STEP * convection
    return convection, next_velocity
```

```python
import functools

import jax
import jax.numpy as jnp
from jax import lax
from jax.experimental import pallas as pl
from jax.experimental.pallas import tpu as pltpu
from jax.sharding import PartitionSpec as P

MESH = pl.DeviceIdType.MESH
SECTION_STEP = 0.5

MODES = 35
SLOT_DEV = 3
CHAOS = 16
GROUP = 32
MODE_PAD = 48
OUT_PAD = 40
JH = 9
LANES = 128
WIDE = 3 * LANES
TABLE_ROWS = JH * OUT_PAD
TABLE_CHUNK = 1024

F32 = jnp.float32
BF16 = jnp.bfloat16


def iota(shape, dim):
    return lax.broadcasted_iota(jnp.int32, shape, dim)


def ring_place(x_hi, chaos):
    y = chaos // 4
    x = 2 * x_hi + (chaos // 2) % 2
    return 2 * (4 * y + x + (y % 2) * (3 - 2 * x)) + chaos % 2


def ring_device(place):
    chip = place // 2
    y = chip // 4
    q = chip % 4
    x = q + (y % 2) * (3 - 2 * q)
    return x // 2, 4 * y + 2 * (x % 2) + place % 2


def dot(a, b, contract=((1,), (0,))):
    return lax.dot_general(a, b, (contract, ((), ())), preferred_element_type=F32)


def kernel(
    space_count,
    velocity_ref,
    slot_ref,
    triples_ref,
    coef_ref,
    out_ref,
    vel,
    send,
    recv,
    field,
    halo_x,
    halo_y,
    table,
    slope,
    weights,
    back,
    home,
    load_sem,
    own_sem,
    send_sem,
    recv_sem,
    halo_send_sem,
    halo_recv_sem,
    back_own_sem,
    back_send_sem,
    back_recv_sem,
):
    space = lax.axis_index("space")
    chaos = lax.axis_index("chaos")
    plane_pair = space // 2
    x_hi = space % 2
    place = ring_place(x_hi, chaos)
    pairs = space_count // 2
    z_up = lax.rem(plane_pair + 1, pairs)
    z_down = lax.rem(plane_pair + pairs - 1, pairs)

    def in_group(other):
        other_hi, other_chaos = ring_device(other)
        return other_hi, other_chaos, (2 * plane_pair + other_hi, other_chaos)

    load = pltpu.make_async_copy(velocity_ref, vel, load_sem)
    load.start()

    barrier = pltpu.get_barrier_semaphore()

    def greet(step, carry):
        _, _, device = in_group(lax.rem(place + step, GROUP))
        pl.semaphore_signal(barrier, inc=1, device_id=device, device_id_type=MESH)
        return carry

    lax.fori_loop(1, GROUP, greet, 0)
    for z in (z_up, z_down):
        pl.semaphore_signal(barrier, inc=1, device_id=(2 * z + x_hi, chaos), device_id_type=MESH)

    row = iota((GROUP * 8, SLOT_DEV * 64), 0)
    col = iota((GROUP * 8, SLOT_DEV * 64), 1)
    spread = (col == ((row // 2) % 4) * 64 + (row // 8) * 2 + row % 2).astype(F32).astype(BF16)
    load.wait()
    values = jnp.concatenate(
        [
            jnp.concatenate([vel[a, d, 0] for d in range(3)], axis=1).astype(BF16)
            for a in range(SLOT_DEV)
        ],
        axis=0,
    )
    send[...] = dot(spread, values).reshape(GROUP, 8, WIDE).astype(BF16)

    pl.semaphore_wait(barrier, GROUP + 1)

    own = pltpu.make_async_copy(send.at[place], recv.at[CHAOS * x_hi + chaos], own_sem)
    own.start()

    def scatter(step, carry):
        other = lax.rem(place + step, GROUP)
        _, _, device = in_group(other)
        pltpu.make_async_remote_copy(
            src_ref=send.at[other],
            dst_ref=recv.at[CHAOS * x_hi + chaos],
            send_sem=send_sem,
            recv_sem=recv_sem,
            device_id=device,
            device_id_type=MESH,
        ).start()
        return carry

    lax.fori_loop(1, GROUP, scatter, 0)

    def add_triples(chunk, carry):
        at = pl.ds(pl.multiple_of(chunk * TABLE_CHUNK, TABLE_CHUNK), TABLE_CHUNK)
        mode_i = triples_ref[0:1, at]
        mode_j = triples_ref[1:2, at]
        mode_k = triples_ref[2:3, at]
        coef = coef_ref[0:1, at].astype(F32)
        high = (mode_j // 4) * OUT_PAD + mode_k
        low = (mode_j % 4) * 64 + mode_i
        left = jnp.where(iota((TABLE_ROWS, TABLE_CHUNK), 0) == high, coef, 0.0).astype(BF16)
        right = jnp.where(iota((256, TABLE_CHUNK), 0) == low, 1.0, 0.0).astype(BF16)
        part = dot(left, right, ((1,), (1,)))
        weights[0:TABLE_ROWS, 0:256] += part
        return carry

    weights[0:TABLE_ROWS, 0:256] = jnp.zeros((TABLE_ROWS, 256), F32)
    lax.fori_loop(0, 4096 // TABLE_CHUNK, add_triples, 0)
    table[...] = weights[0:TABLE_ROWS, 0:256].astype(BF16)

    slots = jnp.broadcast_to(slot_ref[...], (CHAOS * 8, LANES))
    source = iota((CHAOS * 8, LANES), 0)
    hit = (slots == (source // 8) * SLOT_DEV + (source // 2) % 4) & ((source // 2) % 4 < SLOT_DEV)
    hit = hit & (iota((CHAOS * 8, LANES), 1) < MODES)
    gather = [
        jnp.where(hit & (source % 2 == r), 1.0, 0.0)[:, :MODE_PAD] for r in range(2)
    ]
    gather = jnp.concatenate(gather, axis=1)
    to_modes = jnp.concatenate([gather, jnp.zeros((CHAOS * 8, 32), F32)], axis=1).T[: 2 * MODE_PAD]
    to_modes = to_modes.astype(BF16)
    to_slots = gather.astype(BF16)

    own.wait()
    rest = pl.ds(0, GROUP - 1)
    pltpu.make_async_copy(recv.at[rest], recv.at[rest], recv_sem).wait()

    for p in range(2):
        got = recv[p * CHAOS : (p + 1) * CHAOS].astype(F32).reshape(CHAOS * 8, WIDE).astype(BF16)
        modes = dot(to_modes, got).astype(BF16)
        for r in range(2):
            field[p, r] = modes[r * MODE_PAD : (r + 1) * MODE_PAD]

    _, _, ahead = in_group(lax.rem(place + 1, GROUP))
    _, _, behind = in_group(lax.rem(place + GROUP - 1, GROUP))
    below = (2 * z_down + x_hi, chaos)
    above = (2 * z_up + x_hi, chaos)
    halos = [
        (field.at[0], halo_x.at[1], below),
        (field.at[1], halo_x.at[0], above),
        (field.at[:, 0], halo_y.at[1], behind),
        (field.at[:, 1], halo_y.at[0], ahead),
    ]
    halo_copies = [
        pltpu.make_async_remote_copy(
            src_ref=source_ref,
            dst_ref=target_ref,
            send_sem=halo_send_sem.at[n],
            recv_sem=halo_recv_sem.at[n],
            device_id=device,
            device_id_type=MESH,
        )
        for n, (source_ref, target_ref, device) in enumerate(halos)
    ]
    for copy in halo_copies:
        copy.start()

    def put_slope(d, p, r, high, low):
        value = (0.5 * (high - low)).astype(BF16).astype(F32)
        for c in range(3):
            slope[p, r, 3 * d + c] = value[:, c * LANES : (c + 1) * LANES]

    for p in range(2):
        for r in range(2):
            for c in range(3):
                at = slice(c * LANES, (c + 1) * LANES)
                here = field[p, r, :, at].astype(F32)
                slope[p, r, 6 + c] = (
                    (0.5 * (pltpu.roll(here, LANES - 1, 1) - pltpu.roll(here, 1, 1)))
                    .astype(BF16)
                    .astype(F32)
                )

    for copy in halo_copies:
        copy.wait_recv()

    for r in range(2):
        first = field[0, r].astype(F32)
        second = field[1, r].astype(F32)
        put_slope(0, 0, r, second, halo_x[0, r].astype(F32))
        put_slope(0, 1, r, halo_x[1, r].astype(F32), first)
    for p in range(2):
        first = field[p, 0].astype(F32)
        second = field[p, 1].astype(F32)
        put_slope(1, p, 0, second, halo_y[0, p].astype(F32))
        put_slope(1, p, 1, halo_y[1, p].astype(F32), first)

    blank = jnp.zeros((64 - MODE_PAD, WIDE), BF16)
    none = jnp.zeros((64, WIDE), BF16)
    for p in range(2):
        parts = []
        for r in range(2):
            modes = jnp.concatenate([field[p, r], blank], axis=0)
            for jl in range(4):
                pair = [modes, none] if jl % 2 == 0 else [none, modes]
                weights[jl * TABLE_ROWS : (jl + 1) * TABLE_ROWS] = dot(
                    table[:, (jl // 2) * 128 : (jl // 2 + 1) * 128], jnp.concatenate(pair, axis=0)
                )

            def add_mode(jh, sums):
                for jl in range(4):
                    j = jh * 4 + jl
                    rows = pl.ds(pl.multiple_of(jl * TABLE_ROWS + jh * OUT_PAD, 8), OUT_PAD)
                    new = list(sums)
                    for d in range(3):
                        weight = weights[rows, d * LANES : (d + 1) * LANES]
                        for c in range(3):
                            value = slope[p, r, 3 * d + c, pl.ds(j, OUT_PAD, stride=0)]
                            new[c] = new[c] + weight * value
                    sums = tuple(new)
                return sums

            zero = jnp.zeros((OUT_PAD, LANES), F32)
            sums = lax.fori_loop(0, JH, add_mode, (zero, zero, zero))
            part = jnp.concatenate(sums, axis=1)
            parts.append(jnp.concatenate([part, jnp.zeros((8, WIDE), F32)], axis=0).astype(BF16))
        result = jnp.concatenate(parts, axis=0)
        back[p] = dot(to_slots, result).reshape(CHAOS, 8, WIDE).astype(BF16)

        def give(step, carry):
            target = lax.rem(chaos + step, CHAOS)

            @pl.when((target != chaos) | (x_hi != p))
            def _():
                pltpu.make_async_remote_copy(
                    src_ref=back.at[p, target],
                    dst_ref=home.at[place],
                    send_sem=back_send_sem,
                    recv_sem=back_recv_sem,
                    device_id=(2 * plane_pair + p, target),
                    device_id_type=MESH,
                ).start()

            return carry

        lax.fori_loop(0, CHAOS, give, 0)

    own_back = pltpu.make_async_copy(back.at[x_hi, chaos], home.at[place], back_own_sem)
    own_back.start()

    row = iota((SLOT_DEV * 64, GROUP * 8), 0)
    col = iota((SLOT_DEV * 64, GROUP * 8), 1)
    collect = (row == ((col // 2) % 4) * 64 + (col // 8) * 2 + col % 2).astype(F32).astype(BF16)

    own_back.wait()
    pltpu.make_async_copy(home.at[rest], home.at[rest], back_recv_sem).wait()
    got = home[...].astype(F32).reshape(GROUP * 8, WIDE).astype(BF16)
    result = dot(collect, got)
    for a in range(SLOT_DEV):
        for c in range(3):
            out_ref[a, c, 0] = result[a * 64 : (a + 1) * 64, c * LANES : (c + 1) * LANES].astype(BF16)

    pltpu.make_async_copy(send.at[rest], send.at[rest], send_sem).wait()
    for copy in halo_copies:
        copy.wait_send()
    pltpu.make_async_copy(home.at[rest], home.at[rest], back_send_sem).wait()


def on_device(velocity, base_velocity, mode_slot, triples, triple_coef):
    space_count = lax.axis_size("space")
    slots = jnp.pad(mode_slot, (0, LANES - MODES), constant_values=-1).reshape(1, LANES)
    in_vmem = pl.BlockSpec(memory_space=pltpu.VMEM)
    dma = pltpu.SemaphoreType.DMA
    convection = pl.pallas_call(
        functools.partial(kernel, space_count),
        out_shape=jax.ShapeDtypeStruct(velocity.shape, BF16),
        in_specs=[pl.BlockSpec(memory_space=pl.ANY), in_vmem, in_vmem, in_vmem],
        out_specs=in_vmem,
        scratch_shapes=[
            pltpu.VMEM(velocity.shape, F32),
            pltpu.VMEM((GROUP, 8, WIDE), BF16),
            pltpu.VMEM((GROUP, 8, WIDE), BF16),
            pltpu.VMEM((2, 2, MODE_PAD, WIDE), BF16),
            pltpu.VMEM((2, 2, MODE_PAD, WIDE), BF16),
            pltpu.VMEM((2, 2, MODE_PAD, WIDE), BF16),
            pltpu.VMEM((TABLE_ROWS, 256), BF16),
            pltpu.VMEM((2, 2, 9, MODE_PAD, LANES), F32),
            pltpu.VMEM((4 * TABLE_ROWS, WIDE), F32),
            pltpu.VMEM((2, CHAOS, 8, WIDE), BF16),
            pltpu.VMEM((GROUP, 8, WIDE), BF16),
            dma,
            dma,
            dma,
            dma,
            dma((4,)),
            dma((4,)),
            dma,
            dma,
            dma,
        ],
        compiler_params=pltpu.CompilerParams(
            collective_id=0, has_side_effects=True, vmem_limit_bytes=32 * 1024 * 1024
        ),
    )(velocity, slots, triples.T, triple_coef.reshape(1, -1)).astype(F32)
    next_velocity = base_velocity - SECTION_STEP * convection
    return (convection, next_velocity)


def solution(mesh):
    placed = P("chaos", None, "space", None, None)
    return jax.shard_map(
        on_device,
        mesh=mesh,
        in_specs=(placed, placed, P(), P(), P()),
        out_specs=(placed, placed),
        check_vma=False,
    )
```

```python
import functools

import jax
import jax.numpy as jnp
from jax import lax
from jax.experimental import pallas as pl
from jax.experimental.pallas import tpu as pltpu
from jax.sharding import PartitionSpec as P

MESH = pl.DeviceIdType.MESH
SECTION_STEP = 0.5

MODES = 35
SLOT_DEV = 3
CHAOS = 16
GROUP = 32
MODE_PAD = 48
OUT_PAD = 40
JH = 9
LANES = 128
WIDE = 3 * LANES
TABLE_ROWS = JH * OUT_PAD
TABLE_CHUNK = 1024
TRIPLES = 4096

F32 = jnp.float32
BF16 = jnp.bfloat16


def iota(shape, dim):
    return lax.broadcasted_iota(jnp.int32, shape, dim)


def ring_place(x_hi, chaos):
    y = chaos // 4
    x = 2 * x_hi + (chaos // 2) % 2
    return 2 * (4 * y + x + (y % 2) * (3 - 2 * x)) + chaos % 2


def ring_device(place):
    chip = place // 2
    y = chip // 4
    q = chip % 4
    x = q + (y % 2) * (3 - 2 * q)
    return x // 2, 4 * y + 2 * (x % 2) + place % 2


def place_of(member):
    hi = member >> 4
    y = (member >> 2) & 3
    x = 2 * hi + ((member >> 1) & 1)
    return 2 * (4 * y + x + (y & 1) * (3 - 2 * x)) + (member & 1)


def dot(a, b, contract=((1,), (0,))):
    return lax.dot_general(a, b, (contract, ((), ())), preferred_element_type=F32)


def kernel(
    space_count,
    velocity_ref,
    slot_ref,
    triples_ref,
    coef_ref,
    out_ref,
    vel,
    slot_row,
    triples,
    coefs,
    send,
    recv,
    field,
    edge,
    halo_x,
    halo_y,
    sums,
    table,
    slope,
    weights,
    partial,
    back,
    home,
    load_sem,
    own_sem,
    send_sem,
    recv_sem,
    halo_send_sem,
    halo_recv_sem,
    back_own_sem,
    back_send_sem,
    back_recv_sem,
):
    space = lax.axis_index("space")
    chaos = lax.axis_index("chaos")
    plane_pair = space // 2
    x_hi = space % 2
    me = CHAOS * x_hi + chaos
    pairs = space_count // 2
    z_up = lax.rem(plane_pair + 1, pairs)
    z_down = lax.rem(plane_pair + pairs - 1, pairs)

    loads = [
        pltpu.make_async_copy(source_ref, target_ref, load_sem.at[n])
        for n, (source_ref, target_ref) in enumerate(
            [
                (velocity_ref, vel),
                (triples_ref, triples),
                (coef_ref, coefs),
                (slot_ref, slot_row),
            ]
        )
    ]
    for load in loads:
        load.start()

    far = 1 - x_hi
    planes = (far, x_hi)

    def each_member(turn, act):
        def go(step, carry):
            act(planes[turn], lax.rem(chaos + step, CHAOS))
            return carry

        lax.fori_loop(turn, CHAOS, go, 0, unroll=4 if turn == 0 else 5)

    barrier = pltpu.get_barrier_semaphore()

    def greet(hi, other):
        pl.semaphore_signal(
            barrier, inc=1, device_id=(2 * plane_pair + hi, other), device_id_type=MESH
        )

    for turn in range(2):
        each_member(turn, greet)
    for z in (z_up, z_down):
        pl.semaphore_signal(barrier, inc=1, device_id=(2 * z + x_hi, chaos), device_id_type=MESH)

    row = iota((GROUP * 8, LANES), 0)
    source_row = ((row >> 1) & 3) * 64 + place_of(row >> 3) * 2 + (row & 1)
    lane = iota((GROUP * 8, LANES), 1)
    spread = jnp.concatenate(
        [
            jnp.where(source_row == lane, 1.0, 0.0),
            jnp.where(source_row == lane + LANES, 1.0, 0.0)[:, :64],
        ],
        axis=1,
    ).astype(BF16)
    loads[0].wait()
    values = jnp.concatenate(
        [
            jnp.concatenate([vel[a, d, 0] for d in range(3)], axis=1).astype(BF16)
            for a in range(SLOT_DEV)
        ],
        axis=0,
    )
    send[...] = dot(spread, values).reshape(GROUP, 8, WIDE).astype(BF16)

    pl.semaphore_wait(barrier, GROUP + 1)

    def give(hi, other):
        pltpu.make_async_remote_copy(
            src_ref=send.at[CHAOS * hi + other],
            dst_ref=recv.at[me],
            send_sem=send_sem,
            recv_sem=recv_sem,
            device_id=(2 * plane_pair + hi, other),
            device_id_type=MESH,
        ).start()

    for turn in range(2):
        each_member(turn, give)
    own = pltpu.make_async_copy(send.at[me], recv.at[me], own_sem)
    own.start()

    for load in loads[1:]:
        load.wait()

    sums[...] = jnp.zeros((TABLE_ROWS, 256), F32)

    def add_triples(chunk, carry):
        at = pl.ds(pl.multiple_of(chunk * TABLE_CHUNK, TABLE_CHUNK), TABLE_CHUNK)
        mode_i = triples[0:1, at]
        mode_j = triples[1:2, at]
        mode_k = triples[2:3, at]
        eight = coefs[chunk].astype(F32)
        coef = jnp.concatenate([eight[q : q + 1] for q in range(8)], axis=1)
        high = (mode_j >> 2) * OUT_PAD + mode_k
        low = (mode_j & 3) * 64 + mode_i
        left = jnp.where(iota((TABLE_ROWS, TABLE_CHUNK), 0) == high, coef, 0.0).astype(BF16)
        right = jnp.where(iota((256, TABLE_CHUNK), 0) == low, 1.0, 0.0).astype(BF16)
        sums[...] += dot(left, right, ((1,), (1,)))
        return carry

    lax.fori_loop(0, TRIPLES // TABLE_CHUNK, add_triples, 0)
    table[...] = sums[...].astype(BF16)

    source = iota((CHAOS * 8, MODES), 0)
    slot_of = (source >> 3) * SLOT_DEV + ((source >> 1) & 3)
    hit = (slot_row[...] == slot_of) & (((source >> 1) & 3) < SLOT_DEV)
    gap = jnp.zeros((CHAOS * 8, MODE_PAD - MODES), F32)
    gather = []
    for r in range(2):
        gather += [jnp.where(hit & ((source & 1) == r), 1.0, 0.0), gap]
    gather = jnp.concatenate(gather + [jnp.zeros((CHAOS * 8, 32), F32)], axis=1)
    to_modes = gather.T[: 2 * MODE_PAD].astype(BF16)
    to_slots = gather[:, : 2 * MODE_PAD].astype(BF16)

    own.wait()
    rest = pl.ds(0, GROUP - 1)
    pltpu.make_async_copy(recv.at[rest], recv.at[rest], recv_sem).wait()

    for p in range(2):
        got = recv[p * CHAOS : (p + 1) * CHAOS].astype(F32).reshape(CHAOS * 8, WIDE).astype(BF16)
        modes = dot(to_modes, got)
        for r in range(2):
            rows = modes[r * MODE_PAD : (r + 1) * MODE_PAD]
            field[p, r] = rows.astype(BF16)
            edge[p, r] = rows[:OUT_PAD].reshape(OUT_PAD // 8, 8, WIDE).astype(BF16)

    place = ring_place(x_hi, chaos)
    next_hi, next_chaos = ring_device(lax.rem(place + 1, GROUP))
    last_hi, last_chaos = ring_device(lax.rem(place + GROUP - 1, GROUP))
    ahead = (2 * plane_pair + next_hi, next_chaos)
    behind = (2 * plane_pair + last_hi, last_chaos)
    halo_copies = []
    for p in planes:
        up = p * z_down + (1 - p) * z_up
        for r in range(2):
            for kind, source_ref, target_ref, device in (
                (0, edge.at[1 - p, r], halo_x.at[p, r], (2 * up + x_hi, chaos)),
                (1, edge.at[p, 1 - r], halo_y.at[p, r], ahead if r == 0 else behind),
            ):
                halo_copies.append(
                    pltpu.make_async_remote_copy(
                        src_ref=source_ref,
                        dst_ref=target_ref,
                        send_sem=halo_send_sem.at[4 * kind + 2 * p + r],
                        recv_sem=halo_recv_sem.at[4 * kind + 2 * p + r],
                        device_id=device,
                        device_id_type=MESH,
                    )
                )
                halo_copies[-1].start()

    def weigh(n, carry):
        p, r = n >> 1, n & 1
        modes = jnp.concatenate([field[p, r], jnp.zeros((64 - MODE_PAD, WIDE), BF16)], axis=0)
        none = jnp.zeros((64, WIDE), BF16)
        for jl in range(4):
            pair = [modes, none] if jl % 2 == 0 else [none, modes]
            weights[n, jl * TABLE_ROWS : (jl + 1) * TABLE_ROWS] = dot(
                table[:, (jl // 2) * 128 : (jl // 2 + 1) * 128], jnp.concatenate(pair, axis=0)
            )
        for c in range(3):
            here = field[p, r, :, c * LANES : (c + 1) * LANES].astype(F32)[:OUT_PAD]
            turn = pltpu.roll(here, LANES - 1, 1) - pltpu.roll(here, 1, 1)
            slope[n, 6 + c] = (0.5 * turn).astype(BF16).astype(F32)
        return carry

    lax.fori_loop(0, 4, weigh, 0)

    def add_terms(n, directions, start):
        def add_mode(jh, totals):
            totals = list(totals)
            for jl in range(4):
                rows = pl.ds(pl.multiple_of(jl * TABLE_ROWS + jh * OUT_PAD, 8), OUT_PAD)
                for d in directions:
                    weight = weights[n, rows, d * LANES : (d + 1) * LANES]
                    for c in range(3):
                        value = slope[n, 3 * d + c, pl.ds(jh * 4 + jl, OUT_PAD, stride=0)]
                        totals[c] = totals[c] + weight * value
            return tuple(totals)

        return lax.fori_loop(0, JH, add_mode, start)

    def add_z(n, carry):
        zero = jnp.zeros((OUT_PAD, LANES), F32)
        for c, total in enumerate(add_terms(n, (2,), (zero, zero, zero))):
            partial[n, c] = total
        return carry

    lax.fori_loop(0, 4, add_z, 0)

    def values_of(ref, p, r):
        return ref[p, r].astype(F32).reshape(OUT_PAD, WIDE)

    def put_slope(d, n, value):
        value = value.astype(BF16).astype(F32)
        for c in range(3):
            slope[n, 3 * d + c] = value[:, c * LANES : (c + 1) * LANES]

    for turn, p in enumerate(planes):
        half = 0.5 - p.astype(F32)
        rows = []
        for r in range(2):
            n = 2 * p + r
            for copy in halo_copies[4 * turn + 2 * r : 4 * turn + 2 * r + 2]:
                copy.wait_recv()
            put_slope(0, n, half * (values_of(edge, 1 - p, r) - values_of(halo_x, p, r)))
            turned = values_of(edge, p, 1 - r) - values_of(halo_y, p, r)
            put_slope(1, n, (0.5 - r) * turned)
            totals = add_terms(n, (0, 1), tuple(partial[n, c] for c in range(3)))
            rows += [jnp.concatenate(totals, axis=1), jnp.zeros((8, WIDE), F32)]
        result = jnp.concatenate(rows, axis=0).astype(BF16)
        back[p] = dot(to_slots, result).reshape(CHAOS, 8, WIDE).astype(BF16)

        def give_back(hi, other):
            pltpu.make_async_remote_copy(
                src_ref=back.at[hi, other],
                dst_ref=home.at[me],
                send_sem=back_send_sem,
                recv_sem=back_recv_sem,
                device_id=(2 * plane_pair + hi, other),
                device_id_type=MESH,
            ).start()

        each_member(turn, give_back)

    own_back = pltpu.make_async_copy(back.at[x_hi, chaos], home.at[me], back_own_sem)
    own_back.start()

    row = iota((SLOT_DEV * 64, LANES), 0)
    lane = iota((SLOT_DEV * 64, LANES), 1)
    collect = []
    for half in range(2):
        col = lane + half * LANES
        collect.append(
            jnp.where(row == ((col >> 1) & 3) * 64 + place_of(col >> 3) * 2 + (col & 1), 1.0, 0.0)
        )
    collect = jnp.concatenate(collect, axis=1).astype(BF16)

    own_back.wait()
    pltpu.make_async_copy(home.at[rest], home.at[rest], back_recv_sem).wait()
    got = home[...].astype(F32).reshape(GROUP * 8, WIDE).astype(BF16)
    result = dot(collect, got)
    for a in range(SLOT_DEV):
        for c in range(3):
            out_ref[a, c, 0] = result[a * 64 : (a + 1) * 64, c * LANES : (c + 1) * LANES].astype(BF16)

    pltpu.make_async_copy(send.at[rest], send.at[rest], send_sem).wait()
    for copy in halo_copies:
        copy.wait_send()
    pltpu.make_async_copy(home.at[rest], home.at[rest], back_send_sem).wait()


def on_device(velocity, base_velocity, mode_slot, triples, triple_coef):
    space_count = lax.axis_size("space")
    in_hbm = pl.BlockSpec(memory_space=pltpu.HBM)
    operands = (
        velocity,
        mode_slot.reshape(1, MODES),
        triples.T,
        triple_coef.reshape(TRIPLES // TABLE_CHUNK, 8, LANES),
    )
    dma = pltpu.SemaphoreType.DMA
    convection = pl.pallas_call(
        functools.partial(kernel, space_count),
        out_shape=jax.ShapeDtypeStruct(velocity.shape, BF16),
        in_specs=[in_hbm] * 4,
        out_specs=pl.BlockSpec(memory_space=pltpu.VMEM),
        scratch_shapes=[
            pltpu.VMEM(velocity.shape, F32),
            pltpu.VMEM((1, MODES), jnp.int32),
            pltpu.VMEM((3, TRIPLES), jnp.int32),
            pltpu.VMEM((TRIPLES // TABLE_CHUNK, 8, LANES), BF16),
            pltpu.VMEM((GROUP, 8, WIDE), BF16),
            pltpu.VMEM((GROUP, 8, WIDE), BF16),
            pltpu.VMEM((2, 2, MODE_PAD, WIDE), BF16),
            pltpu.VMEM((2, 2, OUT_PAD // 8, 8, WIDE), BF16),
            pltpu.VMEM((2, 2, OUT_PAD // 8, 8, WIDE), BF16),
            pltpu.VMEM((2, 2, OUT_PAD // 8, 8, WIDE), BF16),
            pltpu.VMEM((TABLE_ROWS, 256), F32),
            pltpu.VMEM((TABLE_ROWS, 256), BF16),
            pltpu.VMEM((4, 9, OUT_PAD, LANES), F32),
            pltpu.VMEM((4, 4 * TABLE_ROWS, WIDE), F32),
            pltpu.VMEM((4, 3, OUT_PAD, LANES), F32),
            pltpu.VMEM((2, CHAOS, 8, WIDE), BF16),
            pltpu.VMEM((GROUP, 8, WIDE), BF16),
            dma((4,)),
            dma,
            dma,
            dma,
            dma((8,)),
            dma((8,)),
            dma,
            dma,
            dma,
        ],
        compiler_params=pltpu.CompilerParams(
            collective_id=0, has_side_effects=True, vmem_limit_bytes=40 * 1024 * 1024
        ),
    )(*(pltpu.with_memory_space_constraint(value, pltpu.HBM) for value in operands)).astype(F32)
    next_velocity = base_velocity - SECTION_STEP * convection
    return (convection, next_velocity)


def solution(mesh):
    placed = P("chaos", None, "space", None, None)
    return jax.shard_map(
        on_device,
        mesh=mesh,
        in_specs=(placed, placed, P(), P(), P()),
        out_specs=(placed, placed),
        check_vma=False,
    )
```

```python
import functools

import jax
import jax.numpy as jnp
from jax import lax
from jax.experimental import pallas as pl
from jax.experimental.pallas import tpu as pltpu
from jax.sharding import PartitionSpec as P

MESH = pl.DeviceIdType.MESH
SECTION_STEP = 0.5

MODES = 35
SLOT_DEV = 3
CHAOS = 16
GROUP = 32
MODE_PAD = 48
OUT_PAD = 40
JH = 9
LANES = 128
WIDE = 3 * LANES
TABLE_ROWS = JH * OUT_PAD
TABLE_CHUNK = 1024
TRIPLES = 4096

F32 = jnp.float32
BF16 = jnp.bfloat16


def iota(shape, dim):
    return lax.broadcasted_iota(jnp.int32, shape, dim)


def ring_place(x_hi, chaos):
    y = chaos // 4
    x = 2 * x_hi + (chaos // 2) % 2
    return 2 * (4 * y + x + (y % 2) * (3 - 2 * x)) + chaos % 2


def ring_device(place):
    chip = place // 2
    y = chip // 4
    q = chip % 4
    x = q + (y % 2) * (3 - 2 * q)
    return x // 2, 4 * y + 2 * (x % 2) + place % 2


def place_of(member):
    hi = member >> 4
    y = (member >> 2) & 3
    x = 2 * hi + ((member >> 1) & 1)
    return 2 * (4 * y + x + (y & 1) * (3 - 2 * x)) + (member & 1)


def dot(a, b, contract=((1,), (0,))):
    return lax.dot_general(a, b, (contract, ((), ())), preferred_element_type=F32)


def kernel(
    space_count,
    velocity_ref,
    slot_ref,
    triples_ref,
    coef_ref,
    out_ref,
    vel,
    slot_row,
    triples,
    coefs,
    send,
    recv,
    field,
    edge,
    outer,
    halo_y,
    sums,
    table,
    slope,
    weights,
    partial,
    back,
    home,
    load_sem,
    own_sem,
    send_sem,
    recv_sem,
    ready_sem,
    outer_send_sem,
    outer_recv_sem,
    halo_send_sem,
    halo_recv_sem,
    back_own_sem,
    back_send_sem,
    back_recv_sem,
):
    space = lax.axis_index("space")
    chaos = lax.axis_index("chaos")
    plane_pair = space // 2
    x_hi = space % 2
    me = CHAOS * x_hi + chaos
    pairs = space_count // 2
    z_up = lax.rem(plane_pair + 1, pairs)
    z_down = lax.rem(plane_pair + pairs - 1, pairs)

    loads = [
        pltpu.make_async_copy(source_ref, target_ref, load_sem.at[n])
        for n, (source_ref, target_ref) in enumerate(
            [
                (velocity_ref, vel),
                (triples_ref, triples),
                (coef_ref, coefs),
                (slot_ref, slot_row),
            ]
        )
    ]
    for load in loads:
        load.start()

    far = 1 - x_hi
    planes = (far, x_hi)

    def each_member(turn, act):
        def go(step, carry):
            act(planes[turn], lax.rem(chaos + step, CHAOS))
            return carry

        lax.fori_loop(CHAOS // 2, CHAOS, go, 0, unroll=4)
        lax.fori_loop(turn, CHAOS // 2, go, 0, unroll=4 if turn == 0 else 7)

    barrier = pltpu.get_barrier_semaphore()

    def greet(hi, other):
        pl.semaphore_signal(
            barrier, inc=1, device_id=(2 * plane_pair + hi, other), device_id_type=MESH
        )

    for turn in range(2):
        each_member(turn, greet)
    toward = x_hi * z_up + (1 - x_hi) * z_down
    away = x_hi * z_down + (1 - x_hi) * z_up
    pl.semaphore_signal(barrier, inc=1, device_id=(2 * toward + x_hi, chaos), device_id_type=MESH)

    row = iota((GROUP * 8, LANES), 0)
    source_row = ((row >> 1) & 3) * 64 + place_of(row >> 3) * 2 + (row & 1)
    lane = iota((GROUP * 8, LANES), 1)
    spread = jnp.concatenate(
        [
            jnp.where(source_row == lane, 1.0, 0.0),
            jnp.where(source_row == lane + LANES, 1.0, 0.0)[:, :64],
        ],
        axis=1,
    ).astype(BF16)
    loads[0].wait()
    values = jnp.concatenate(
        [
            jnp.concatenate([vel[a, d, 0] for d in range(3)], axis=1).astype(BF16)
            for a in range(SLOT_DEV)
        ],
        axis=0,
    )
    send[...] = dot(spread, values).reshape(GROUP, 8, WIDE).astype(BF16)

    def give_halos():
        pl.semaphore_wait(ready_sem, 1)
        for hi in planes:

            def give_halo(step, carry):
                other = lax.rem(chaos + step, CHAOS)
                pltpu.make_async_remote_copy(
                    src_ref=send.at[CHAOS * hi + other],
                    dst_ref=outer.at[far, chaos],
                    send_sem=outer_send_sem,
                    recv_sem=outer_recv_sem.at[far],
                    device_id=(2 * toward + hi, other),
                    device_id_type=MESH,
                ).start()
                return carry

            lax.fori_loop(0, CHAOS, give_halo, 0, unroll=4)

    pl.semaphore_wait(barrier, GROUP)
    pl.semaphore_signal(ready_sem, inc=1, device_id=(2 * away + x_hi, chaos), device_id_type=MESH)

    @pl.when(toward == 0)
    def _():
        give_halos()

    def give(hi, other):
        pltpu.make_async_remote_copy(
            src_ref=send.at[CHAOS * hi + other],
            dst_ref=recv.at[me],
            send_sem=send_sem,
            recv_sem=recv_sem,
            device_id=(2 * plane_pair + hi, other),
            device_id_type=MESH,
        ).start()

    for turn in range(2):
        each_member(turn, give)
    own = pltpu.make_async_copy(send.at[me], recv.at[me], own_sem)
    own.start()

    @pl.when(toward != 0)
    def _():
        give_halos()

    for load in loads[1:]:
        load.wait()

    sums[...] = jnp.zeros((TABLE_ROWS, 256), F32)

    def add_triples(chunk, carry):
        at = pl.ds(pl.multiple_of(chunk * TABLE_CHUNK, TABLE_CHUNK), TABLE_CHUNK)
        mode_i = triples[0:1, at]
        mode_j = triples[1:2, at]
        mode_k = triples[2:3, at]
        eight = coefs[chunk].astype(F32)
        coef = jnp.concatenate([eight[q : q + 1] for q in range(8)], axis=1)
        high = (mode_j >> 2) * OUT_PAD + mode_k
        low = (mode_j & 3) * 64 + mode_i
        left = jnp.where(iota((TABLE_ROWS, TABLE_CHUNK), 0) == high, coef, 0.0).astype(BF16)
        right = jnp.where(iota((256, TABLE_CHUNK), 0) == low, 1.0, 0.0).astype(BF16)
        sums[...] += dot(left, right, ((1,), (1,)))
        return carry

    lax.fori_loop(0, TRIPLES // TABLE_CHUNK, add_triples, 0)
    table[...] = sums[...].astype(BF16)

    source = iota((CHAOS * 8, MODES), 0)
    slot_of = (source >> 3) * SLOT_DEV + ((source >> 1) & 3)
    hit = (slot_row[...] == slot_of) & (((source >> 1) & 3) < SLOT_DEV)
    gap = jnp.zeros((CHAOS * 8, MODE_PAD - MODES), F32)
    gather = []
    for r in range(2):
        gather += [jnp.where(hit & ((source & 1) == r), 1.0, 0.0), gap]
    gather = jnp.concatenate(gather + [jnp.zeros((CHAOS * 8, 32), F32)], axis=1)
    to_modes = gather.T[: 2 * MODE_PAD].astype(BF16)
    to_slots = gather[:, : 2 * MODE_PAD].astype(BF16)

    own.wait()
    rest = pl.ds(0, GROUP - 1)
    pltpu.make_async_copy(recv.at[rest], recv.at[rest], recv_sem).wait()

    for p in range(2):
        got = recv[p * CHAOS : (p + 1) * CHAOS].astype(F32).reshape(CHAOS * 8, WIDE).astype(BF16)
        modes = dot(to_modes, got)
        for r in range(2):
            rows = modes[r * MODE_PAD : (r + 1) * MODE_PAD]
            field[p, r] = rows.astype(BF16)
            edge[p, r] = rows[:OUT_PAD].reshape(OUT_PAD // 8, 8, WIDE).astype(BF16)

    place = ring_place(x_hi, chaos)
    next_hi, next_chaos = ring_device(lax.rem(place + 1, GROUP))
    last_hi, last_chaos = ring_device(lax.rem(place + GROUP - 1, GROUP))
    ahead = (2 * plane_pair + next_hi, next_chaos)
    behind = (2 * plane_pair + last_hi, last_chaos)
    halo_copies = []
    for p in planes:
        for r in range(2):
            halo_copies.append(
                pltpu.make_async_remote_copy(
                    src_ref=edge.at[p, 1 - r],
                    dst_ref=halo_y.at[p, r],
                    send_sem=halo_send_sem.at[2 * p + r],
                    recv_sem=halo_recv_sem.at[2 * p + r],
                    device_id=ahead if r == 0 else behind,
                    device_id_type=MESH,
                )
            )
            halo_copies[-1].start()

    def weigh(n, carry):
        p, r = n >> 1, n & 1
        modes = jnp.concatenate([field[p, r], jnp.zeros((64 - MODE_PAD, WIDE), BF16)], axis=0)
        none = jnp.zeros((64, WIDE), BF16)
        for jl in range(4):
            pair = [modes, none] if jl % 2 == 0 else [none, modes]
            weights[n, jl * TABLE_ROWS : (jl + 1) * TABLE_ROWS] = dot(
                table[:, (jl // 2) * 128 : (jl // 2 + 1) * 128], jnp.concatenate(pair, axis=0)
            )
        for c in range(3):
            here = field[p, r, :, c * LANES : (c + 1) * LANES].astype(F32)[:OUT_PAD]
            turn = pltpu.roll(here, LANES - 1, 1) - pltpu.roll(here, 1, 1)
            slope[n, 6 + c] = (0.5 * turn).astype(BF16).astype(F32)
        return carry

    lax.fori_loop(0, 4, weigh, 0)

    def add_terms(n, directions, start):
        def add_mode(jh, totals):
            totals = list(totals)
            for jl in range(4):
                rows = pl.ds(pl.multiple_of(jl * TABLE_ROWS + jh * OUT_PAD, 8), OUT_PAD)
                for d in directions:
                    weight = weights[n, rows, d * LANES : (d + 1) * LANES]
                    for c in range(3):
                        value = slope[n, 3 * d + c, pl.ds(jh * 4 + jl, OUT_PAD, stride=0)]
                        totals[c] = totals[c] + weight * value
            return tuple(totals)

        return lax.fori_loop(0, JH, add_mode, start)

    def add_z(n, carry):
        zero = jnp.zeros((OUT_PAD, LANES), F32)
        for c, total in enumerate(add_terms(n, (2,), (zero, zero, zero))):
            partial[n, c] = total
        return carry

    lax.fori_loop(0, 4, add_z, 0)

    def values_of(ref, p, r):
        return ref[p, r].astype(F32).reshape(OUT_PAD, WIDE)

    def put_slope(d, n, value):
        value = value.astype(BF16).astype(F32)
        for c in range(3):
            slope[n, 3 * d + c] = value[:, c * LANES : (c + 1) * LANES]

    for turn, p in enumerate(planes):
        half = 0.5 - p.astype(F32)
        pltpu.make_async_copy(outer.at[p], outer.at[p], outer_recv_sem.at[p]).wait()
        beyond = dot(to_modes, outer[p].astype(F32).reshape(CHAOS * 8, WIDE).astype(BF16))
        rows = []
        for r in range(2):
            n = 2 * p + r
            halo_copies[2 * turn + r].wait_recv()
            outside = beyond[r * MODE_PAD : r * MODE_PAD + OUT_PAD]
            put_slope(0, n, half * (values_of(edge, 1 - p, r) - outside))
            turned = values_of(edge, p, 1 - r) - values_of(halo_y, p, r)
            put_slope(1, n, (0.5 - r) * turned)
            totals = add_terms(n, (0, 1), tuple(partial[n, c] for c in range(3)))
            rows += [jnp.concatenate(totals, axis=1), jnp.zeros((8, WIDE), F32)]
        result = jnp.concatenate(rows, axis=0).astype(BF16)
        back[p] = dot(to_slots, result).reshape(CHAOS, 8, WIDE).astype(BF16)

        def give_back(hi, other):
            pltpu.make_async_remote_copy(
                src_ref=back.at[hi, other],
                dst_ref=home.at[me],
                send_sem=back_send_sem,
                recv_sem=back_recv_sem,
                device_id=(2 * plane_pair + hi, other),
                device_id_type=MESH,
            ).start()

        each_member(turn, give_back)

    own_back = pltpu.make_async_copy(back.at[x_hi, chaos], home.at[me], back_own_sem)
    own_back.start()

    row = iota((SLOT_DEV * 64, LANES), 0)
    lane = iota((SLOT_DEV * 64, LANES), 1)
    collect = []
    for half in range(2):
        col = lane + half * LANES
        collect.append(
            jnp.where(row == ((col >> 1) & 3) * 64 + place_of(col >> 3) * 2 + (col & 1), 1.0, 0.0)
        )
    collect = jnp.concatenate(collect, axis=1).astype(BF16)

    own_back.wait()
    pltpu.make_async_copy(home.at[rest], home.at[rest], back_recv_sem).wait()
    got = home[...].astype(F32).reshape(GROUP * 8, WIDE).astype(BF16)
    result = dot(collect, got)
    for a in range(SLOT_DEV):
        for c in range(3):
            out_ref[a, c, 0] = result[a * 64 : (a + 1) * 64, c * LANES : (c + 1) * LANES].astype(BF16)

    pltpu.make_async_copy(send.at[rest], send.at[rest], send_sem).wait()
    pltpu.make_async_copy(send, send, outer_send_sem).wait()
    for copy in halo_copies:
        copy.wait_send()
    pltpu.make_async_copy(home.at[rest], home.at[rest], back_send_sem).wait()


def on_device(velocity, base_velocity, mode_slot, triples, triple_coef):
    space_count = lax.axis_size("space")
    in_hbm = pl.BlockSpec(memory_space=pltpu.HBM)
    operands = (
        velocity,
        mode_slot.reshape(1, MODES),
        triples.T,
        triple_coef.reshape(TRIPLES // TABLE_CHUNK, 8, LANES),
    )
    dma = pltpu.SemaphoreType.DMA
    convection = pl.pallas_call(
        functools.partial(kernel, space_count),
        out_shape=jax.ShapeDtypeStruct(velocity.shape, BF16),
        in_specs=[in_hbm] * 4,
        out_specs=pl.BlockSpec(memory_space=pltpu.VMEM),
        scratch_shapes=[
            pltpu.VMEM(velocity.shape, F32),
            pltpu.VMEM((1, MODES), jnp.int32),
            pltpu.VMEM((3, TRIPLES), jnp.int32),
            pltpu.VMEM((TRIPLES // TABLE_CHUNK, 8, LANES), BF16),
            pltpu.VMEM((GROUP, 8, WIDE), BF16),
            pltpu.VMEM((GROUP, 8, WIDE), BF16),
            pltpu.VMEM((2, 2, MODE_PAD, WIDE), BF16),
            pltpu.VMEM((2, 2, OUT_PAD // 8, 8, WIDE), BF16),
            pltpu.VMEM((2, CHAOS, 8, WIDE), BF16),
            pltpu.VMEM((2, 2, OUT_PAD // 8, 8, WIDE), BF16),
            pltpu.VMEM((TABLE_ROWS, 256), F32),
            pltpu.VMEM((TABLE_ROWS, 256), BF16),
            pltpu.VMEM((4, 9, OUT_PAD, LANES), F32),
            pltpu.VMEM((4, 4 * TABLE_ROWS, WIDE), F32),
            pltpu.VMEM((4, 3, OUT_PAD, LANES), F32),
            pltpu.VMEM((2, CHAOS, 8, WIDE), BF16),
            pltpu.VMEM((GROUP, 8, WIDE), BF16),
            dma((4,)),
            dma,
            dma,
            dma,
            pltpu.SemaphoreType.REGULAR,
            dma,
            dma((2,)),
            dma((4,)),
            dma((4,)),
            dma,
            dma,
            dma,
        ],
        compiler_params=pltpu.CompilerParams(
            collective_id=0, has_side_effects=True, vmem_limit_bytes=40 * 1024 * 1024
        ),
    )(*(pltpu.with_memory_space_constraint(value, pltpu.HBM) for value in operands)).astype(F32)
    next_velocity = base_velocity - SECTION_STEP * convection
    return (convection, next_velocity)


def solution(mesh):
    placed = P("chaos", None, "space", None, None)
    return jax.shard_map(
        on_device,
        mesh=mesh,
        in_specs=(placed, placed, P(), P(), P()),
        out_specs=(placed, placed),
        check_vma=False,
    )
```

```python
import functools

import jax
import jax.numpy as jnp
from jax import lax
from jax.experimental import pallas as pl
from jax.experimental.pallas import tpu as pltpu
from jax.sharding import PartitionSpec as P

MESH = pl.DeviceIdType.MESH
SECTION_STEP = 0.5

MODES = 35
SLOT_DEV = 3
CHAOS = 16
GROUP = 32
MODE_PAD = 48
OUT_PAD = 40
JH = 9
LANES = 128
WIDE = 3 * LANES
USED = pl.ds(0, 2 * SLOT_DEV)
TABLE_ROWS = JH * OUT_PAD
TABLE_CHUNK = 1024
TRIPLES = 4096

F32 = jnp.float32
BF16 = jnp.bfloat16


def iota(shape, dim):
    return lax.broadcasted_iota(jnp.int32, shape, dim)


def ring_place(x_hi, chaos):
    y = chaos // 4
    x = 2 * x_hi + (chaos // 2) % 2
    return 2 * (4 * y + x + (y % 2) * (3 - 2 * x)) + chaos % 2


def ring_device(place):
    chip = place // 2
    y = chip // 4
    q = chip % 4
    x = q + (y % 2) * (3 - 2 * q)
    return x // 2, 4 * y + 2 * (x % 2) + place % 2


def place_of(member):
    hi = member >> 4
    y = (member >> 2) & 3
    x = 2 * hi + ((member >> 1) & 1)
    return 2 * (4 * y + x + (y & 1) * (3 - 2 * x)) + (member & 1)


def dot(a, b, contract=((1,), (0,))):
    return lax.dot_general(a, b, (contract, ((), ())), preferred_element_type=F32)


def kernel(
    space_count,
    velocity_ref,
    slot_ref,
    triples_ref,
    coef_ref,
    out_ref,
    vel,
    slot_row,
    triples,
    coefs,
    send,
    recv,
    field,
    edge,
    outer,
    halo_y,
    sums,
    table,
    slope,
    weights,
    partial,
    back,
    home,
    load_sem,
    own_sem,
    send_sem,
    recv_sem,
    ready_sem,
    outer_send_sem,
    outer_recv_sem,
    halo_send_sem,
    halo_recv_sem,
    back_own_sem,
    back_send_sem,
    back_recv_sem,
):
    space = lax.axis_index("space")
    chaos = lax.axis_index("chaos")
    plane_pair = space // 2
    x_hi = space % 2
    me = CHAOS * x_hi + chaos
    pairs = space_count // 2
    z_up = lax.rem(plane_pair + 1, pairs)
    z_down = lax.rem(plane_pair + pairs - 1, pairs)

    loads = [
        pltpu.make_async_copy(source_ref, target_ref, load_sem.at[n])
        for n, (source_ref, target_ref) in enumerate(
            [
                (velocity_ref, vel),
                (triples_ref, triples),
                (coef_ref, coefs),
                (slot_ref, slot_row),
            ]
        )
    ]
    for load in loads:
        load.start()

    far = 1 - x_hi
    planes = (far, x_hi)

    def each_member(turn, act):
        def go(step, carry):
            act(planes[turn], lax.rem(chaos + step, CHAOS))
            return carry

        lax.fori_loop(CHAOS // 2, CHAOS, go, 0, unroll=4)
        lax.fori_loop(turn, CHAOS // 2, go, 0, unroll=4 if turn == 0 else 7)

    recv[...] = jnp.zeros(recv.shape, BF16)
    outer[...] = jnp.zeros(outer.shape, BF16)
    home[...] = jnp.zeros(home.shape, BF16)

    barrier = pltpu.get_barrier_semaphore()

    def greet(hi, other):
        pl.semaphore_signal(
            barrier, inc=1, device_id=(2 * plane_pair + hi, other), device_id_type=MESH
        )

    for turn in range(2):
        each_member(turn, greet)
    toward = x_hi * z_up + (1 - x_hi) * z_down
    away = x_hi * z_down + (1 - x_hi) * z_up
    pl.semaphore_signal(barrier, inc=1, device_id=(2 * toward + x_hi, chaos), device_id_type=MESH)

    row = iota((GROUP * 8, LANES), 0)
    source_row = ((row >> 1) & 3) * 64 + place_of(row >> 3) * 2 + (row & 1)
    lane = iota((GROUP * 8, LANES), 1)
    spread = jnp.concatenate(
        [
            jnp.where(source_row == lane, 1.0, 0.0),
            jnp.where(source_row == lane + LANES, 1.0, 0.0)[:, :64],
        ],
        axis=1,
    ).astype(BF16)
    loads[0].wait()
    values = jnp.concatenate(
        [
            jnp.concatenate([vel[a, d, 0] for d in range(3)], axis=1).astype(BF16)
            for a in range(SLOT_DEV)
        ],
        axis=0,
    )
    send[...] = dot(spread, values).reshape(GROUP, 8, WIDE).astype(BF16)

    def give_halos():
        pl.semaphore_wait(ready_sem, 1)
        for hi in planes:

            def give_halo(step, carry):
                other = lax.rem(chaos + step, CHAOS)
                pltpu.make_async_remote_copy(
                    src_ref=send.at[CHAOS * hi + other, USED],
                    dst_ref=outer.at[far, chaos, USED],
                    send_sem=outer_send_sem,
                    recv_sem=outer_recv_sem.at[far],
                    device_id=(2 * toward + hi, other),
                    device_id_type=MESH,
                ).start()
                return carry

            lax.fori_loop(0, CHAOS, give_halo, 0, unroll=4)

    pl.semaphore_wait(barrier, GROUP)
    pl.semaphore_signal(ready_sem, inc=1, device_id=(2 * away + x_hi, chaos), device_id_type=MESH)

    @pl.when(toward == 0)
    def _():
        give_halos()

    def give(hi, other):
        pltpu.make_async_remote_copy(
            src_ref=send.at[CHAOS * hi + other, USED],
            dst_ref=recv.at[me, USED],
            send_sem=send_sem,
            recv_sem=recv_sem,
            device_id=(2 * plane_pair + hi, other),
            device_id_type=MESH,
        ).start()

    for turn in range(2):
        each_member(turn, give)
    own = pltpu.make_async_copy(send.at[me], recv.at[me], own_sem)
    own.start()

    @pl.when(toward != 0)
    def _():
        give_halos()

    for load in loads[1:]:
        load.wait()

    sums[...] = jnp.zeros((TABLE_ROWS, 256), F32)

    def add_triples(chunk, carry):
        at = pl.ds(pl.multiple_of(chunk * TABLE_CHUNK, TABLE_CHUNK), TABLE_CHUNK)
        mode_i = triples[0:1, at]
        mode_j = triples[1:2, at]
        mode_k = triples[2:3, at]
        eight = coefs[chunk].astype(F32)
        coef = jnp.concatenate([eight[q : q + 1] for q in range(8)], axis=1)
        high = (mode_j >> 2) * OUT_PAD + mode_k
        low = (mode_j & 3) * 64 + mode_i
        left = jnp.where(iota((TABLE_ROWS, TABLE_CHUNK), 0) == high, coef, 0.0).astype(BF16)
        right = jnp.where(iota((256, TABLE_CHUNK), 0) == low, 1.0, 0.0).astype(BF16)
        sums[...] += dot(left, right, ((1,), (1,)))
        return carry

    lax.fori_loop(0, TRIPLES // TABLE_CHUNK, add_triples, 0)
    table[...] = sums[...].astype(BF16)

    source = iota((CHAOS * 8, MODES), 0)
    slot_of = (source >> 3) * SLOT_DEV + ((source >> 1) & 3)
    hit = (slot_row[...] == slot_of) & (((source >> 1) & 3) < SLOT_DEV)
    gap = jnp.zeros((CHAOS * 8, MODE_PAD - MODES), F32)
    gather = []
    for r in range(2):
        gather += [jnp.where(hit & ((source & 1) == r), 1.0, 0.0), gap]
    gather = jnp.concatenate(gather + [jnp.zeros((CHAOS * 8, 32), F32)], axis=1)
    to_modes = gather.T[: 2 * MODE_PAD].astype(BF16)
    to_slots = gather[:, : 2 * MODE_PAD].astype(BF16)

    own.wait()
    rest = pl.ds(0, GROUP - 1)
    pltpu.make_async_copy(recv.at[rest, USED], recv.at[rest, USED], recv_sem).wait()

    for p in range(2):
        got = recv[p * CHAOS : (p + 1) * CHAOS].astype(F32).reshape(CHAOS * 8, WIDE).astype(BF16)
        modes = dot(to_modes, got)
        for r in range(2):
            rows = modes[r * MODE_PAD : (r + 1) * MODE_PAD]
            field[p, r] = rows.astype(BF16)
            edge[p, r] = rows[:OUT_PAD].reshape(OUT_PAD // 8, 8, WIDE).astype(BF16)

    place = ring_place(x_hi, chaos)
    next_hi, next_chaos = ring_device(lax.rem(place + 1, GROUP))
    last_hi, last_chaos = ring_device(lax.rem(place + GROUP - 1, GROUP))
    ahead = (2 * plane_pair + next_hi, next_chaos)
    behind = (2 * plane_pair + last_hi, last_chaos)
    halo_copies = []
    for p in planes:
        for r in range(2):
            halo_copies.append(
                pltpu.make_async_remote_copy(
                    src_ref=edge.at[p, 1 - r],
                    dst_ref=halo_y.at[p, r],
                    send_sem=halo_send_sem.at[2 * p + r],
                    recv_sem=halo_recv_sem.at[2 * p + r],
                    device_id=ahead if r == 0 else behind,
                    device_id_type=MESH,
                )
            )
            halo_copies[-1].start()

    def weigh(n, carry):
        p, r = n >> 1, n & 1
        modes = jnp.concatenate([field[p, r], jnp.zeros((64 - MODE_PAD, WIDE), BF16)], axis=0)
        none = jnp.zeros((64, WIDE), BF16)
        for jl in range(4):
            pair = [modes, none] if jl % 2 == 0 else [none, modes]
            weights[n, jl * TABLE_ROWS : (jl + 1) * TABLE_ROWS] = dot(
                table[:, (jl // 2) * 128 : (jl // 2 + 1) * 128], jnp.concatenate(pair, axis=0)
            )
        for c in range(3):
            here = field[p, r, :, c * LANES : (c + 1) * LANES].astype(F32)[:OUT_PAD]
            turn = pltpu.roll(here, LANES - 1, 1) - pltpu.roll(here, 1, 1)
            slope[n, 6 + c] = (0.5 * turn).astype(BF16).astype(F32)
        return carry

    lax.fori_loop(0, 4, weigh, 0)

    def add_terms(n, directions, start):
        def add_mode(jh, totals):
            totals = list(totals)
            for jl in range(4):
                rows = pl.ds(pl.multiple_of(jl * TABLE_ROWS + jh * OUT_PAD, 8), OUT_PAD)
                for d in directions:
                    weight = weights[n, rows, d * LANES : (d + 1) * LANES]
                    for c in range(3):
                        value = slope[n, 3 * d + c, pl.ds(jh * 4 + jl, OUT_PAD, stride=0)]
                        totals[c] = totals[c] + weight * value
            return tuple(totals)

        return lax.fori_loop(0, JH, add_mode, start)

    def add_z(n, carry):
        zero = jnp.zeros((OUT_PAD, LANES), F32)
        for c, total in enumerate(add_terms(n, (2,), (zero, zero, zero))):
            partial[n, c] = total
        return carry

    lax.fori_loop(0, 4, add_z, 0)

    def values_of(ref, p, r):
        return ref[p, r].astype(F32).reshape(OUT_PAD, WIDE)

    def put_slope(d, n, value):
        value = value.astype(BF16).astype(F32)
        for c in range(3):
            slope[n, 3 * d + c] = value[:, c * LANES : (c + 1) * LANES]

    for turn, p in enumerate(planes):
        half = 0.5 - p.astype(F32)
        pltpu.make_async_copy(outer.at[p, :, USED], outer.at[p, :, USED], outer_recv_sem.at[p]).wait()
        beyond = dot(to_modes, outer[p].astype(F32).reshape(CHAOS * 8, WIDE).astype(BF16))
        rows = []
        for r in range(2):
            n = 2 * p + r
            halo_copies[2 * turn + r].wait_recv()
            outside = beyond[r * MODE_PAD : r * MODE_PAD + OUT_PAD]
            put_slope(0, n, half * (values_of(edge, 1 - p, r) - outside))
            turned = values_of(edge, p, 1 - r) - values_of(halo_y, p, r)
            put_slope(1, n, (0.5 - r) * turned)
            totals = add_terms(n, (0, 1), tuple(partial[n, c] for c in range(3)))
            rows += [jnp.concatenate(totals, axis=1), jnp.zeros((8, WIDE), F32)]
        result = jnp.concatenate(rows, axis=0).astype(BF16)
        back[p] = dot(to_slots, result).reshape(CHAOS, 8, WIDE).astype(BF16)

        def give_back(hi, other):
            pltpu.make_async_remote_copy(
                src_ref=back.at[hi, other, USED],
                dst_ref=home.at[me, USED],
                send_sem=back_send_sem,
                recv_sem=back_recv_sem,
                device_id=(2 * plane_pair + hi, other),
                device_id_type=MESH,
            ).start()

        each_member(turn, give_back)

    own_back = pltpu.make_async_copy(back.at[x_hi, chaos], home.at[me], back_own_sem)
    own_back.start()

    row = iota((SLOT_DEV * 64, LANES), 0)
    lane = iota((SLOT_DEV * 64, LANES), 1)
    collect = []
    for half in range(2):
        col = lane + half * LANES
        collect.append(
            jnp.where(row == ((col >> 1) & 3) * 64 + place_of(col >> 3) * 2 + (col & 1), 1.0, 0.0)
        )
    collect = jnp.concatenate(collect, axis=1).astype(BF16)

    own_back.wait()
    pltpu.make_async_copy(home.at[rest, USED], home.at[rest, USED], back_recv_sem).wait()
    got = home[...].astype(F32).reshape(GROUP * 8, WIDE).astype(BF16)
    result = dot(collect, got)
    for a in range(SLOT_DEV):
        for c in range(3):
            out_ref[a, c, 0] = result[a * 64 : (a + 1) * 64, c * LANES : (c + 1) * LANES].astype(BF16)

    pltpu.make_async_copy(send.at[rest, USED], send.at[rest, USED], send_sem).wait()
    pltpu.make_async_copy(send.at[:, USED], send.at[:, USED], outer_send_sem).wait()
    for copy in halo_copies:
        copy.wait_send()
    pltpu.make_async_copy(home.at[rest, USED], home.at[rest, USED], back_send_sem).wait()


def on_device(velocity, base_velocity, mode_slot, triples, triple_coef):
    space_count = lax.axis_size("space")
    in_hbm = pl.BlockSpec(memory_space=pltpu.HBM)
    operands = (
        velocity,
        mode_slot.reshape(1, MODES),
        triples.T,
        triple_coef.reshape(TRIPLES // TABLE_CHUNK, 8, LANES),
    )
    dma = pltpu.SemaphoreType.DMA
    convection = pl.pallas_call(
        functools.partial(kernel, space_count),
        out_shape=jax.ShapeDtypeStruct(velocity.shape, BF16),
        in_specs=[in_hbm] * 4,
        out_specs=pl.BlockSpec(memory_space=pltpu.VMEM),
        scratch_shapes=[
            pltpu.VMEM(velocity.shape, F32),
            pltpu.VMEM((1, MODES), jnp.int32),
            pltpu.VMEM((3, TRIPLES), jnp.int32),
            pltpu.VMEM((TRIPLES // TABLE_CHUNK, 8, LANES), BF16),
            pltpu.VMEM((GROUP, 8, WIDE), BF16),
            pltpu.VMEM((GROUP, 8, WIDE), BF16),
            pltpu.VMEM((2, 2, MODE_PAD, WIDE), BF16),
            pltpu.VMEM((2, 2, OUT_PAD // 8, 8, WIDE), BF16),
            pltpu.VMEM((2, CHAOS, 8, WIDE), BF16),
            pltpu.VMEM((2, 2, OUT_PAD // 8, 8, WIDE), BF16),
            pltpu.VMEM((TABLE_ROWS, 256), F32),
            pltpu.VMEM((TABLE_ROWS, 256), BF16),
            pltpu.VMEM((4, 9, OUT_PAD, LANES), F32),
            pltpu.VMEM((4, 4 * TABLE_ROWS, WIDE), F32),
            pltpu.VMEM((4, 3, OUT_PAD, LANES), F32),
            pltpu.VMEM((2, CHAOS, 8, WIDE), BF16),
            pltpu.VMEM((GROUP, 8, WIDE), BF16),
            dma((4,)),
            dma,
            dma,
            dma,
            pltpu.SemaphoreType.REGULAR,
            dma,
            dma((2,)),
            dma((4,)),
            dma((4,)),
            dma,
            dma,
            dma,
        ],
        compiler_params=pltpu.CompilerParams(
            collective_id=0, has_side_effects=True, vmem_limit_bytes=40 * 1024 * 1024
        ),
    )(*(pltpu.with_memory_space_constraint(value, pltpu.HBM) for value in operands)).astype(F32)
    next_velocity = base_velocity - SECTION_STEP * convection
    return (convection, next_velocity)


def solution(mesh):
    placed = P("chaos", None, "space", None, None)
    return jax.shard_map(
        on_device,
        mesh=mesh,
        in_specs=(placed, placed, P(), P(), P()),
        out_specs=(placed, placed),
        check_vma=False,
    )
```

```python
import functools

import jax
import jax.numpy as jnp
from jax import lax
from jax.experimental import pallas as pl
from jax.experimental.pallas import tpu as pltpu
from jax.sharding import PartitionSpec as P

MESH = pl.DeviceIdType.MESH
SECTION_STEP = 0.5

MODES = 35
SLOT_DEV = 3
CHAOS = 16
GROUP = 32
MODE_PAD = 48
OUT_PAD = 40
JH = 9
LANES = 128
WIDE = 3 * LANES
USED = pl.ds(0, 2 * SLOT_DEV)
TABLE_ROWS = JH * OUT_PAD
TABLE_CHUNK = 1024
TRIPLES = 4096

F32 = jnp.float32
BF16 = jnp.bfloat16


def iota(shape, dim):
    return lax.broadcasted_iota(jnp.int32, shape, dim)


def ring_place(x_hi, chaos):
    y = chaos // 4
    x = 2 * x_hi + (chaos // 2) % 2
    return 2 * (4 * y + x + (y % 2) * (3 - 2 * x)) + chaos % 2


def ring_device(place):
    chip = place // 2
    y = chip // 4
    q = chip % 4
    x = q + (y % 2) * (3 - 2 * q)
    return x // 2, 4 * y + 2 * (x % 2) + place % 2


def place_of(member):
    hi = member >> 4
    y = (member >> 2) & 3
    x = 2 * hi + ((member >> 1) & 1)
    return 2 * (4 * y + x + (y & 1) * (3 - 2 * x)) + (member & 1)


def dot(a, b, contract=((1,), (0,))):
    return lax.dot_general(a, b, (contract, ((), ())), preferred_element_type=F32)


def kernel(
    space_count,
    velocity_ref,
    slot_ref,
    triples_ref,
    coef_ref,
    out_ref,
    vel,
    slot_row,
    triples,
    coefs,
    send,
    recv,
    field,
    edge,
    outer,
    halo_y,
    sums,
    table,
    slope,
    weights,
    partial,
    back,
    home,
    load_sem,
    own_sem,
    send_sem,
    recv_sem,
    ready_sem,
    outer_send_sem,
    outer_recv_sem,
    halo_send_sem,
    halo_recv_sem,
    back_own_sem,
    back_send_sem,
    back_recv_sem,
):
    space = lax.axis_index("space")
    chaos = lax.axis_index("chaos")
    plane_pair = space // 2
    x_hi = space % 2
    me = CHAOS * x_hi + chaos
    pairs = space_count // 2
    z_up = lax.rem(plane_pair + 1, pairs)
    z_down = lax.rem(plane_pair + pairs - 1, pairs)

    loads = [
        pltpu.make_async_copy(source_ref, target_ref, load_sem.at[n])
        for n, (source_ref, target_ref) in enumerate(
            [
                (velocity_ref, vel),
                (triples_ref, triples),
                (coef_ref, coefs),
                (slot_ref, slot_row),
            ]
        )
    ]
    for load in loads:
        load.start()

    far = 1 - x_hi
    planes = (far, x_hi)

    def each_member(turn, act):
        def go(step, carry):
            act(planes[turn], lax.rem(chaos + step, CHAOS))
            return carry

        lax.fori_loop(CHAOS // 2, CHAOS, go, 0, unroll=4)
        lax.fori_loop(turn, CHAOS // 2, go, 0, unroll=4 if turn == 0 else 7)

    barrier = pltpu.get_barrier_semaphore()
    toward = x_hi * z_up + (1 - x_hi) * z_down
    away = x_hi * z_down + (1 - x_hi) * z_up
    pl.semaphore_signal(barrier, inc=1, device_id=(2 * toward + x_hi, chaos), device_id_type=MESH)

    recv[...] = jnp.zeros(recv.shape, BF16)
    outer[...] = jnp.zeros(outer.shape, BF16)

    def greet(hi, other):
        pl.semaphore_signal(
            barrier, inc=1, device_id=(2 * plane_pair + hi, other), device_id_type=MESH
        )

    for turn in range(2):
        each_member(turn, greet)
    home[...] = jnp.zeros(home.shape, BF16)

    row = iota((GROUP * 8, LANES), 0)
    source_row = ((row >> 1) & 3) * 64 + place_of(row >> 3) * 2 + (row & 1)
    lane = iota((GROUP * 8, LANES), 1)
    spread = jnp.concatenate(
        [
            jnp.where(source_row == lane, 1.0, 0.0),
            jnp.where(source_row == lane + LANES, 1.0, 0.0)[:, :64],
        ],
        axis=1,
    ).astype(BF16)
    loads[0].wait()
    values = jnp.concatenate(
        [
            jnp.concatenate([vel[a, d, 0] for d in range(3)], axis=1).astype(BF16)
            for a in range(SLOT_DEV)
        ],
        axis=0,
    )
    send[...] = dot(spread, values).reshape(GROUP, 8, WIDE).astype(BF16)

    def give_halos():
        pl.semaphore_wait(ready_sem, 1)
        for hi in planes:

            def give_halo(step, carry):
                other = lax.rem(chaos + step, CHAOS)
                pltpu.make_async_remote_copy(
                    src_ref=send.at[CHAOS * hi + other, USED],
                    dst_ref=outer.at[far, chaos, USED],
                    send_sem=outer_send_sem,
                    recv_sem=outer_recv_sem.at[far],
                    device_id=(2 * toward + hi, other),
                    device_id_type=MESH,
                ).start()
                return carry

            lax.fori_loop(0, CHAOS, give_halo, 0, unroll=4)

    pl.semaphore_wait(barrier, GROUP)
    pl.semaphore_signal(ready_sem, inc=1, device_id=(2 * away + x_hi, chaos), device_id_type=MESH)

    @pl.when(toward == 0)
    def _():
        give_halos()

    def give(hi, other):
        pltpu.make_async_remote_copy(
            src_ref=send.at[CHAOS * hi + other, USED],
            dst_ref=recv.at[me, USED],
            send_sem=send_sem,
            recv_sem=recv_sem,
            device_id=(2 * plane_pair + hi, other),
            device_id_type=MESH,
        ).start()

    for turn in range(2):
        each_member(turn, give)
    own = pltpu.make_async_copy(send.at[me], recv.at[me], own_sem)
    own.start()

    @pl.when(toward != 0)
    def _():
        give_halos()

    for load in loads[1:]:
        load.wait()

    sums[...] = jnp.zeros((TABLE_ROWS, 256), F32)

    def add_triples(chunk, carry):
        at = pl.ds(pl.multiple_of(chunk * TABLE_CHUNK, TABLE_CHUNK), TABLE_CHUNK)
        mode_i = triples[0:1, at]
        mode_j = triples[1:2, at]
        mode_k = triples[2:3, at]
        eight = coefs[chunk].astype(F32)
        coef = jnp.concatenate([eight[q : q + 1] for q in range(8)], axis=1)
        high = (mode_j >> 2) * OUT_PAD + mode_k
        low = (mode_j & 3) * 64 + mode_i
        left = jnp.where(iota((TABLE_ROWS, TABLE_CHUNK), 0) == high, coef, 0.0).astype(BF16)
        right = jnp.where(iota((256, TABLE_CHUNK), 0) == low, 1.0, 0.0).astype(BF16)
        sums[...] += dot(left, right, ((1,), (1,)))
        return carry

    lax.fori_loop(0, TRIPLES // TABLE_CHUNK, add_triples, 0)
    table[...] = sums[...].astype(BF16)

    source = iota((CHAOS * 8, MODES), 0)
    slot_of = (source >> 3) * SLOT_DEV + ((source >> 1) & 3)
    hit = (slot_row[...] == slot_of) & (((source >> 1) & 3) < SLOT_DEV)
    gap = jnp.zeros((CHAOS * 8, MODE_PAD - MODES), F32)
    gather = []
    for r in range(2):
        gather += [jnp.where(hit & ((source & 1) == r), 1.0, 0.0), gap]
    gather = jnp.concatenate(gather + [jnp.zeros((CHAOS * 8, 32), F32)], axis=1)
    to_modes = gather.T[: 2 * MODE_PAD].astype(BF16)
    to_slots = gather[:, : 2 * MODE_PAD].astype(BF16)

    own.wait()
    rest = pl.ds(0, GROUP - 1)
    pltpu.make_async_copy(recv.at[rest, USED], recv.at[rest, USED], recv_sem).wait()

    for p in range(2):
        got = recv[p * CHAOS : (p + 1) * CHAOS].astype(F32).reshape(CHAOS * 8, WIDE).astype(BF16)
        modes = dot(to_modes, got)
        for r in range(2):
            rows = modes[r * MODE_PAD : (r + 1) * MODE_PAD]
            field[p, r] = rows.astype(BF16)
            edge[p, r] = rows[:OUT_PAD].reshape(OUT_PAD // 8, 8, WIDE).astype(BF16)

    place = ring_place(x_hi, chaos)
    next_hi, next_chaos = ring_device(lax.rem(place + 1, GROUP))
    last_hi, last_chaos = ring_device(lax.rem(place + GROUP - 1, GROUP))
    ahead = (2 * plane_pair + next_hi, next_chaos)
    behind = (2 * plane_pair + last_hi, last_chaos)
    halo_copies = []
    for p in planes:
        for r in range(2):
            halo_copies.append(
                pltpu.make_async_remote_copy(
                    src_ref=edge.at[p, 1 - r],
                    dst_ref=halo_y.at[p, r],
                    send_sem=halo_send_sem.at[2 * p + r],
                    recv_sem=halo_recv_sem.at[2 * p + r],
                    device_id=ahead if r == 0 else behind,
                    device_id_type=MESH,
                )
            )
            halo_copies[-1].start()

    def weigh(n, carry):
        p, r = n >> 1, n & 1
        modes = jnp.concatenate([field[p, r], jnp.zeros((64 - MODE_PAD, WIDE), BF16)], axis=0)
        none = jnp.zeros((64, WIDE), BF16)
        for jl in range(4):
            pair = [modes, none] if jl % 2 == 0 else [none, modes]
            weights[n, jl * TABLE_ROWS : (jl + 1) * TABLE_ROWS] = dot(
                table[:, (jl // 2) * 128 : (jl // 2 + 1) * 128], jnp.concatenate(pair, axis=0)
            )
        for c in range(3):
            here = field[p, r, :, c * LANES : (c + 1) * LANES].astype(F32)[:OUT_PAD]
            turn = pltpu.roll(here, LANES - 1, 1) - pltpu.roll(here, 1, 1)
            slope[n, 6 + c] = (0.5 * turn).astype(BF16).astype(F32)
        return carry

    lax.fori_loop(0, 4, weigh, 0)

    def add_terms(n, directions, start):
        def add_mode(jh, totals):
            totals = list(totals)
            for jl in range(4):
                rows = pl.ds(pl.multiple_of(jl * TABLE_ROWS + jh * OUT_PAD, 8), OUT_PAD)
                for d in directions:
                    weight = weights[n, rows, d * LANES : (d + 1) * LANES]
                    for c in range(3):
                        value = slope[n, 3 * d + c, pl.ds(jh * 4 + jl, OUT_PAD, stride=0)]
                        totals[c] = totals[c] + weight * value
            return tuple(totals)

        return lax.fori_loop(0, JH, add_mode, start)

    def add_z(n, carry):
        zero = jnp.zeros((OUT_PAD, LANES), F32)
        for c, total in enumerate(add_terms(n, (2,), (zero, zero, zero))):
            partial[n, c] = total
        return carry

    lax.fori_loop(0, 4, add_z, 0)

    def values_of(ref, p, r):
        return ref[p, r].astype(F32).reshape(OUT_PAD, WIDE)

    def put_slope(d, n, value):
        value = value.astype(BF16).astype(F32)
        for c in range(3):
            slope[n, 3 * d + c] = value[:, c * LANES : (c + 1) * LANES]

    for turn, p in enumerate(planes):
        half = 0.5 - p.astype(F32)
        pltpu.make_async_copy(outer.at[p, :, USED], outer.at[p, :, USED], outer_recv_sem.at[p]).wait()
        beyond = dot(to_modes, outer[p].astype(F32).reshape(CHAOS * 8, WIDE).astype(BF16))
        rows = []
        for r in range(2):
            n = 2 * p + r
            halo_copies[2 * turn + r].wait_recv()
            outside = beyond[r * MODE_PAD : r * MODE_PAD + OUT_PAD]
            put_slope(0, n, half * (values_of(edge, 1 - p, r) - outside))
            turned = values_of(edge, p, 1 - r) - values_of(halo_y, p, r)
            put_slope(1, n, (0.5 - r) * turned)
            totals = add_terms(n, (0, 1), tuple(partial[n, c] for c in range(3)))
            rows += [jnp.concatenate(totals, axis=1), jnp.zeros((8, WIDE), F32)]
        result = jnp.concatenate(rows, axis=0).astype(BF16)
        back[p] = dot(to_slots, result).reshape(CHAOS, 8, WIDE).astype(BF16)

        def give_back(hi, other):
            pltpu.make_async_remote_copy(
                src_ref=back.at[hi, other, USED],
                dst_ref=home.at[me, USED],
                send_sem=back_send_sem,
                recv_sem=back_recv_sem,
                device_id=(2 * plane_pair + hi, other),
                device_id_type=MESH,
            ).start()

        each_member(turn, give_back)

    own_back = pltpu.make_async_copy(back.at[x_hi, chaos], home.at[me], back_own_sem)
    own_back.start()

    row = iota((SLOT_DEV * 64, LANES), 0)
    lane = iota((SLOT_DEV * 64, LANES), 1)
    collect = []
    for half in range(2):
        col = lane + half * LANES
        collect.append(
            jnp.where(row == ((col >> 1) & 3) * 64 + place_of(col >> 3) * 2 + (col & 1), 1.0, 0.0)
        )
    collect = jnp.concatenate(collect, axis=1).astype(BF16)

    own_back.wait()
    pltpu.make_async_copy(home.at[rest, USED], home.at[rest, USED], back_recv_sem).wait()
    got = home[...].astype(F32).reshape(GROUP * 8, WIDE).astype(BF16)
    result = dot(collect, got)
    for a in range(SLOT_DEV):
        for c in range(3):
            out_ref[a, c, 0] = result[a * 64 : (a + 1) * 64, c * LANES : (c + 1) * LANES].astype(BF16)

    pltpu.make_async_copy(send.at[rest, USED], send.at[rest, USED], send_sem).wait()
    pltpu.make_async_copy(send.at[:, USED], send.at[:, USED], outer_send_sem).wait()
    for copy in halo_copies:
        copy.wait_send()
    pltpu.make_async_copy(home.at[rest, USED], home.at[rest, USED], back_send_sem).wait()


def on_device(velocity, base_velocity, mode_slot, triples, triple_coef):
    space_count = lax.axis_size("space")
    in_hbm = pl.BlockSpec(memory_space=pltpu.HBM)
    operands = (
        velocity,
        mode_slot.reshape(1, MODES),
        triples.T,
        triple_coef.reshape(TRIPLES // TABLE_CHUNK, 8, LANES),
    )
    dma = pltpu.SemaphoreType.DMA
    convection = pl.pallas_call(
        functools.partial(kernel, space_count),
        out_shape=jax.ShapeDtypeStruct(velocity.shape, BF16),
        in_specs=[in_hbm] * 4,
        out_specs=pl.BlockSpec(memory_space=pltpu.VMEM),
        scratch_shapes=[
            pltpu.VMEM(velocity.shape, F32),
            pltpu.VMEM((1, MODES), jnp.int32),
            pltpu.VMEM((3, TRIPLES), jnp.int32),
            pltpu.VMEM((TRIPLES // TABLE_CHUNK, 8, LANES), BF16),
            pltpu.VMEM((GROUP, 8, WIDE), BF16),
            pltpu.VMEM((GROUP, 8, WIDE), BF16),
            pltpu.VMEM((2, 2, MODE_PAD, WIDE), BF16),
            pltpu.VMEM((2, 2, OUT_PAD // 8, 8, WIDE), BF16),
            pltpu.VMEM((2, CHAOS, 8, WIDE), BF16),
            pltpu.VMEM((2, 2, OUT_PAD // 8, 8, WIDE), BF16),
            pltpu.VMEM((TABLE_ROWS, 256), F32),
            pltpu.VMEM((TABLE_ROWS, 256), BF16),
            pltpu.VMEM((4, 9, OUT_PAD, LANES), F32),
            pltpu.VMEM((4, 4 * TABLE_ROWS, WIDE), F32),
            pltpu.VMEM((4, 3, OUT_PAD, LANES), F32),
            pltpu.VMEM((2, CHAOS, 8, WIDE), BF16),
            pltpu.VMEM((GROUP, 8, WIDE), BF16),
            dma((4,)),
            dma,
            dma,
            dma,
            pltpu.SemaphoreType.REGULAR,
            dma,
            dma((2,)),
            dma((4,)),
            dma((4,)),
            dma,
            dma,
            dma,
        ],
        compiler_params=pltpu.CompilerParams(
            collective_id=0, has_side_effects=True, vmem_limit_bytes=40 * 1024 * 1024
        ),
    )(*(pltpu.with_memory_space_constraint(value, pltpu.HBM) for value in operands)).astype(F32)
    next_velocity = base_velocity - SECTION_STEP * convection
    return (convection, next_velocity)


def solution(mesh):
    placed = P("chaos", None, "space", None, None)
    return jax.shard_map(
        on_device,
        mesh=mesh,
        in_specs=(placed, placed, P(), P(), P()),
        out_specs=(placed, placed),
        check_vma=False,
    )
```
